32 devices in a mesh: view: 4 (over y, x), point: 8 (over z, core).
Axes of the slice: x: 2, y: 2, z: 4, core: 2. Of those that a mesh axis runs over, the one named last changes fastest.
Arguments:
- features: bfloat16 [128, 32, 128, 256], P(('view', 'point')), may hold values from -6 to 6
- tiles: int32 [128, 2], P(('view', 'point')), may hold values from 0 to 7, as said below
- masks: int32 [128, 32, 128], P(('view', 'point')), may hold values from 0 to 1
- w_self: bfloat16 [3, 256, 256], replicated, may hold values from -0.375 to 0.375
- w_col: bfloat16 [3, 256, 256], replicated, may hold values from -0.09375 to 0.09375
- w_row: bfloat16 [3, 256, 256], replicated, may hold values from -0.03125 to 0.03125
- bias: float32 [3, 256], replicated, may hold values from -3 to 3
Outputs:
- result: bfloat16 [128, 32, 128, 256], P(('view', 'point'))
The draws below stay inside these ranges and needn't reach their ends.
Inputs may be any that keep to these rules, and one draw needn't show every extreme that they name: `tiles`: column 0 is a view tile of the slot's own view block, below 4. Column 1 below 4 is a point tile of the device's own point block; otherwise, minus 4, a point tile of the block of the next device along point, the last device's next being the first. No two slots name the same tile.
All inputs are finite; a program needn't handle non-finite values.
Results may differ from the reference program's by a relative error of at most 0.0051.
Values sent between devices are 32-bit elements; how exact they have to be, the bound alone decides.
A program may use at most 128 MiB of HBM per device.

```python
import jax
import jax.numpy as jnp
from jax import lax

D = 256
TV = 32
TP = 128
VT_DEV = 4
PT_DEV = 4
SLOTS = 4
LAYERS = 3
ALL_SLOTS = 128
N_VIEW = 4
N_POINT = 8


def tile_layout(key):
    base_key = jax.random.fold_in(key, 7)
    help_key, order_key = jax.random.split(base_key)
    cell_total = VT_DEV * PT_DEV
    helped = jax.random.randint(help_key, (N_VIEW, N_POINT), 0, SLOTS + 1).astype(jnp.int32)
    order_keys = jax.random.split(order_key, N_VIEW * N_POINT)
    cell_order = jax.vmap(lambda subkey: jax.random.permutation(subkey, cell_total))(order_keys)
    cell_order = cell_order.reshape(N_VIEW, N_POINT, cell_total).astype(jnp.int32)
    helped_after = jnp.roll(helped, -1, axis=1)
    owned = SLOTS - helped_after
    slot_index = jnp.arange(SLOTS, dtype=jnp.int32)[None, None, :]
    is_owned = slot_index < owned[..., None]
    own_pick = jnp.minimum(helped[..., None] + slot_index, cell_total - 1)
    after_pick = jnp.maximum(slot_index - owned[..., None], 0)
    order_after = jnp.roll(cell_order, -1, axis=1)
    own_cell = jnp.take_along_axis(cell_order, own_pick, axis=2)
    after_cell = jnp.take_along_axis(order_after, after_pick, axis=2)
    chosen = jnp.where(is_owned, own_cell, after_cell)
    offset = jnp.where(is_owned, 0, PT_DEV)
    view_column = chosen // PT_DEV
    point_column = chosen % PT_DEV + offset
    stacked = jnp.stack([view_column, point_column], axis=-1)
    return stacked.reshape(N_VIEW * N_POINT * SLOTS, 2).astype(jnp.int32)


def draw_tiles(key, part):
    return tile_layout(key)


def draw_masks(key, part):
    slot_ids = jnp.arange(ALL_SLOTS, dtype=jnp.int32)
    device_index = slot_ids // SLOTS
    view_pos = device_index // N_POINT
    point_pos = device_index % N_POINT
    threshold = 150 + 350 * point_pos // max(N_POINT - 1, 1) + 350 * view_pos // max(N_VIEW - 1, 1)
    drawn = jax.random.randint(jax.random.fold_in(key, 3), (ALL_SLOTS, TV, TP), 0, 1000)
    return (drawn < threshold[:, None, None]).astype(jnp.int32)


def block_scale(stream_key, shape, cuts, least, top_value):
    def one(axis_at, shards_of):
        steps = jax.random.uniform(jax.random.fold_in(jax.random.fold_in(stream_key, 6), axis_at), (shards_of,), jnp.float32, least / len(cuts), top_value / len(cuts))
        return jnp.repeat(jnp.exp(steps), shape[axis_at] // shards_of).reshape((-1,) + (1,) * (len(shape) - axis_at - 1))

    loudness = one(*cuts[0])
    for cut in cuts[1:]:
        loudness = loudness * one(*cut)
    return loudness


def scatter_about(stream_key, shape, width, reach, pieces=(), held_as=jnp.bfloat16):
    entries = jax.random.normal(stream_key, shape, jnp.float32) * width
    if len(pieces) > 0:
        entries = block_scale(stream_key, shape, pieces, -0.22, 0.18) * entries
    return jnp.clip(entries, min=-reach, max=reach).astype(held_as)


def setup_inputs(seed: int = 0) -> dict:
    seeds = jax.random.split(jax.random.key(seed), 8)
    return {
        "features": scatter_about(seeds[0], (ALL_SLOTS, TV, TP, D), 1.0, 6.0, ((0, 32),)),
        "tiles": draw_tiles(jax.random.fold_in(seeds[7], 71), 0),
        "masks": draw_masks(jax.random.fold_in(seeds[7], 71), 0),
        "w_self": scatter_about(seeds[3], (LAYERS, D, D), D ** -0.5, 0.375),
        "w_col": scatter_about(seeds[4], (LAYERS, D, D), (D * 16) ** -0.5, 0.09375),
        "w_row": scatter_about(seeds[5], (LAYERS, D, D), (D * 128) ** -0.5, 0.03125),
        "bias": scatter_about(seeds[6], (LAYERS, D), 0.5, 3.0, (), jnp.float32),
    }


def reference(features, tiles, masks, w_self, w_col, w_row, bias):
    device_index = jnp.arange(ALL_SLOTS, dtype=jnp.int32) // SLOTS
    view_pos = device_index // N_POINT
    point_pos = device_index % N_POINT
    view_tile = (view_pos * VT_DEV + tiles[:, 0]).astype(jnp.int32)
    point_tile = ((point_pos + tiles[:, 1] // PT_DEV) % N_POINT * PT_DEV + tiles[:, 1] % PT_DEV).astype(jnp.int32)
    view_tiles_all = VT_DEV * N_VIEW
    point_tiles_all = PT_DEV * N_POINT
    mask_f = masks.astype(jnp.float32)
    row_count = jax.ops.segment_sum(lax.optimization_barrier(jnp.sum(mask_f, axis=2)), view_tile, view_tiles_all)
    col_count = jax.ops.segment_sum(lax.optimization_barrier(jnp.sum(mask_f, axis=1)), point_tile, point_tiles_all)
    row_scale = 1.0 / jnp.sqrt(jnp.maximum(row_count, 1.0))
    col_scale = 1.0 / jnp.sqrt(jnp.maximum(col_count, 1.0))
    devices_all = ALL_SLOTS // SLOTS
    mask_blocks = masks.reshape(devices_all, SLOTS, TV, TP)
    view_blocks = view_tile.reshape(devices_all, SLOTS)
    point_blocks = point_tile.reshape(devices_all, SLOTS)
    current = features
    for layer_step in range(LAYERS):
        feat_blocks = current.reshape(devices_all, SLOTS, TV, TP, D)

        def slot_sums(block_args):
            block_feat, block_mask = block_args
            feat32 = block_feat.astype(jnp.float32)
            mask32 = block_mask.astype(jnp.float32)
            row_part = jnp.einsum('src,srcd->srd', mask32, feat32)
            col_part = jnp.einsum('src,srcd->scd', mask32, feat32)
            return (row_part, col_part)
        row_part, col_part = lax.map(slot_sums, (feat_blocks, mask_blocks))
        row_sum = jax.ops.segment_sum(row_part.reshape(ALL_SLOTS, TV, D), view_tile, view_tiles_all)
        col_sum = jax.ops.segment_sum(col_part.reshape(ALL_SLOTS, TP, D), point_tile, point_tiles_all)
        row_term = (row_sum * row_scale[..., None]).astype(jnp.bfloat16)
        col_term = (col_sum * col_scale[..., None]).astype(jnp.bfloat16)
        row_proj = jnp.dot(row_term.reshape(-1, D), w_row[layer_step], preferred_element_type=jnp.float32).reshape(view_tiles_all, TV, D)
        col_proj = jnp.dot(col_term.reshape(-1, D), w_col[layer_step], preferred_element_type=jnp.float32).reshape(point_tiles_all, TP, D)
        weight_self = w_self[layer_step]
        bias_row = bias[layer_step]

        def layer_block(block_args):
            block_feat, block_mask, block_view, block_point = block_args
            self_proj = jnp.dot(block_feat.reshape(-1, D), weight_self, preferred_element_type=jnp.float32).reshape(SLOTS, TV, TP, D)
            mixed_sum = self_proj + col_proj[block_point][:, None, :, :] + row_proj[block_view][:, :, None, :] + bias_row
            return (jnp.maximum(mixed_sum, 0.0) * block_mask.astype(jnp.float32)[..., None]).astype(jnp.bfloat16)
        current = lax.map(layer_block, (feat_blocks, mask_blocks, view_blocks, point_blocks)).reshape(ALL_SLOTS, TV, TP, D)
    return current
```

```python
import functools

import jax
import jax.numpy as jnp
from jax import lax
from jax.experimental import pallas as pl
from jax.experimental.pallas import tpu as pltpu
from jax.sharding import PartitionSpec as P

VT_DEV = 4
PT_DEV = 4
MESH = pl.DeviceIdType.MESH
F32 = jnp.float32
BF16 = jnp.bfloat16


def wide(x, width):
    reps = width // x.shape[-1]
    return x if reps == 1 else jnp.concatenate([x] * reps, axis=-1)


def exchange_kernel(
    nv, np_, nk,
    tiles_ref, feat_ref, mask_ref, wself_ref, wcol_ref, wrow_ref, bias_ref,
    cur_out, colp_out, rowp_out,
    cur, mask_t, col_send, rs_buf, f_send, f_buf, own_acc, b_send, b_buf, ag_send, ag_buf,
    row_acc, row_send, row_rs, row_ag_send, row_ag, row_p,
    ci_send, ci_buf, cf_send, cf_buf, ri_send, ri_buf, col_scale, row_scale, q_all,
    feat_sem, out_sem, rs_s, rs_r, f_s, f_r, b_s, b_r, ag_s, ag_r,
    rr_s, rr_r, ra_s, ra_r, ci_s, ci_r, cf_s, cf_r, ri_s, ri_r,
):
    a = lax.axis_index("view")
    b = lax.axis_index("point")
    slots, rows, cols, width = cur.shape
    layers = wself_ref.shape[0]
    chunk = cols // nk
    part = chunk // nv
    share = row_send.shape[1]
    nxt = lax.rem(b + 1, np_)
    prv = lax.rem(b + np_ - 1, np_)

    def remote(src, dst, ssem, rsem, va, pb):
        return pltpu.make_async_remote_copy(
            src_ref=src, dst_ref=dst, send_sem=ssem, recv_sem=rsem,
            device_id=(va, pb), device_id_type=MESH,
        )

    def view_at(o):
        return lax.rem(a + o, nv)

    def point_at(o):
        return lax.rem(b + o, np_)

    def rs_copy(k, o):
        return remote(col_send.at[k, view_at(o)], rs_buf.at[k, o - 1],
                      rs_s.at[k, o - 1], rs_r.at[k, o - 1], view_at(o), b)

    def ag_copy(k, o):
        return remote(ag_send.at[k, o - 1], ag_buf.at[k, o],
                      ag_s.at[k, o - 1], ag_r.at[k, o - 1], view_at(o), b)

    def f_copy(k):
        return remote(f_send.at[k], f_buf.at[k], f_s.at[k], f_r.at[k], a, nxt)

    def b_copy(k):
        return remote(b_send.at[k], b_buf.at[k], b_s.at[k], b_r.at[k], a, prv)

    def rr_copy(o):
        return remote(row_send.at[point_at(o)], row_rs.at[o - 1],
                      rr_s.at[o - 1], rr_r.at[o - 1], a, point_at(o))

    def ra_copy(o):
        return remote(row_ag_send, row_ag.at[o - 1], ra_s.at[o - 1], ra_r.at[o - 1], a, point_at(o))

    def ci_copy(o):
        return remote(ci_send.at[view_at(o)], ci_buf.at[o - 1],
                      ci_s.at[o - 1], ci_r.at[o - 1], view_at(o), b)

    def cf_copy():
        return remote(cf_send, cf_buf, cf_s.at[0], cf_r.at[0], a, nxt)

    def ri_copy(o):
        return remote(ri_send.at[point_at(o)], ri_buf.at[o - 1],
                      ri_s.at[o - 1], ri_r.at[o - 1], a, point_at(o))

    def feat_copy(k):
        span = pl.ds(k * chunk, chunk)
        return pltpu.make_async_copy(
            feat_ref.at[:, :, span, :], cur.at[:, :, span, :], feat_sem.at[k])

    for k in range(nk):
        feat_copy(k).start()

    barrier = pltpu.get_barrier_semaphore()
    for o in range(1, nv):
        pl.semaphore_signal(barrier, inc=1, device_id=(view_at(o), b), device_id_type=MESH)
    for o in range(1, np_):
        pl.semaphore_signal(barrier, inc=1, device_id=(a, point_at(o)), device_id_type=MESH)

    lanes = ci_send.shape[-1]
    per_part = nk * part
    for s in range(slots):
        m = mask_ref[s].astype(F32)
        mt = m.T
        mask_t[s] = mt
        ccount = jnp.broadcast_to(jnp.sum(mt, axis=1, keepdims=True), (cols, lanes))
        q = jnp.full((8, lanes), tiles_ref[s, 1], jnp.int32).astype(F32)
        for j in range(nv):
            for k in range(nk):
                at = k * chunk + j * part
                ci_send[j, s, k * part:(k + 1) * part, :] = ccount[at:at + part]
            ci_send[j, s, per_part:, :] = q
    for v in range(VT_DEV):
        total = jnp.zeros((rows, lanes), F32)
        for s in range(slots):
            rcount = jnp.broadcast_to(
                jnp.sum(mask_ref[s].astype(F32), axis=1, keepdims=True), (rows, lanes))
            hit = jnp.full((rows, lanes), tiles_ref[s, 0], jnp.int32) == v
            total = total + jnp.where(hit, rcount, 0.0)
        for i in range(max(rows // share, 1)):
            at = v * rows + i * share
            ri_send[at // share] = total[i * share:(i + 1) * share]

    pl.semaphore_wait(barrier, nv - 1 + np_ - 1)
    for o in range(1, nv):
        ci_copy(o).start()
    for o in range(1, np_):
        ri_copy(o).start()

    def sum_rows(k, s, group, value_of):
        span = pl.ds(k * chunk, chunk)
        mk = mask_t[s, span, :]
        col = jnp.zeros((chunk, width), F32)
        for g in range(rows // group):
            values = value_of(g)
            sums = []
            for i in range(group):
                r = g * group + i
                y = values(i, jnp.broadcast_to(mk[:, r:r + 1], (chunk, width)))
                col = col + y
                sums.append(jnp.sum(y, axis=0, keepdims=True))
            new = jnp.concatenate(sums, axis=0)
            at = pl.ds(g * group, group)
            if k == 0:
                row_acc[s, at, :] = new
            else:
                row_acc[s, at, :] = row_acc[s, at, :] + new
        for j in range(nv):
            col_send[k, j, s] = col[j * part:(j + 1) * part]

    group = 8

    def first_sums(k):
        span = pl.ds(k * chunk, chunk)

        def slot(s, carry):
            def value_of(g):
                return lambda i, m: cur[s, g * group + i, span, :].astype(F32) * m
            sum_rows(k, s, group, value_of)
            return carry
        lax.fori_loop(0, slots, slot, 0)

    def layer_chunk(layer, k):
        span = pl.ds(k * chunk, chunk)

        def slot(s, carry):
            colp = jnp.concatenate(
                [ag_buf[k, lax.rem(a - j + nv, nv), s] for j in range(nv)], axis=0)
            v = tiles_ref[s, 0]
            rowp = row_p[v]

            def value_of(g):
                x = cur[s, g * group:(g + 1) * group, span, :].reshape(group * chunk, width)
                z = jnp.dot(x, wself_ref[layer], preferred_element_type=F32)

                def one(i, m):
                    r = g * group + i
                    y = z[i * chunk:(i + 1) * chunk] + colp + rowp[r:r + 1, :]
                    y = (jnp.maximum(y, 0.0) * m).astype(BF16)
                    cur[s, r, span, :] = y
                    return y.astype(F32)
                return one
            sum_rows(k, s, group, value_of)
            return carry
        lax.fori_loop(0, slots, slot, 0)

    def send_rows():
        for v in range(VT_DEV):
            total = jnp.zeros((rows, width), F32)
            for s in range(slots):
                hit = jnp.full((rows, width), tiles_ref[s, 0], jnp.int32) == v
                total = total + jnp.where(hit, row_acc[s], 0.0)
            for i in range(max(rows // share, 1)):
                at = v * rows + i * share
                row_send[at // share] = total[i * share:(i + 1) * share]
        for o in range(1, np_):
            rr_copy(o).start()

    def send_cols(k):
        for o in range(1, nv):
            rs_copy(k, o).start()

    def picked(q, t, block):
        return jnp.where(q == float(t), block, 0.0)

    for k in range(nk):
        feat_copy(k).wait()
        first_sums(k)
        send_cols(k)
    send_rows()

    for o in range(1, nv):
        ci_copy(o).wait()
    for s in range(slots):
        q_all[0, s] = wide(ci_send[a, s, per_part:, :], width)
        for o in range(1, nv):
            q_all[o, s] = wide(ci_buf[o - 1, s, per_part:, :], width)
    own = []
    for t in range(2 * PT_DEV):
        total = jnp.zeros((per_part, lanes), F32)
        for s in range(slots):
            for o in range(nv):
                block = ci_send.at[a] if o == 0 else ci_buf.at[o - 1]
                q = jnp.concatenate([block[s, per_part:, :]] * (per_part // 8), axis=0)
                total = total + picked(q, t, block[s, :per_part, :])
        if t < PT_DEV:
            col_scale[t] = total
        else:
            cf_send[t - PT_DEV] = total
    cf_copy().start()
    for o in range(1, np_):
        ri_copy(o).wait()
    total = ri_send[b]
    for o in range(1, np_):
        total = total + ri_buf[o - 1]
    row_scale[...] = wide(1.0 / jnp.sqrt(jnp.maximum(total, 1.0)), width)
    cf_copy().wait()
    for t in range(PT_DEV):
        total = col_scale[t] + cf_buf[t]
        col_scale[t] = 1.0 / jnp.sqrt(jnp.maximum(total, 1.0))

    def stage_sum(layer, k):
        for o in range(1, nv):
            rs_copy(k, o).wait()
        for t in range(2 * PT_DEV):
            total = jnp.zeros((part, width), F32)
            for o in range(nv):
                for s in range(slots):
                    block = col_send[k, a, s] if o == 0 else rs_buf[k, o - 1, s]
                    q = jnp.concatenate([q_all[o, s]] * (part // 8), axis=0)
                    total = total + picked(q, t, block)
            if t < PT_DEV:
                own_acc[k, t] = total
            else:
                f_send[k, t - PT_DEV] = total
        f_copy(k).start()

    def stage_project(layer, k):
        f_copy(k).wait()
        scale = wide(col_scale[:, k * part:(k + 1) * part, :], width)
        term = ((own_acc[k] + f_buf[k]) * scale).reshape(PT_DEV * part, width).astype(BF16)
        out = jnp.dot(term, wcol_ref[layer], preferred_element_type=F32)
        b_send[k] = out.reshape(PT_DEV, part, width)
        b_copy(k).start()

    def stage_choose(layer, k):
        b_copy(k).wait()
        for o in range(nv):
            for s in range(slots):
                q = jnp.concatenate([q_all[(nv - o) % nv, s]] * (part // 8), axis=0)
                total = jnp.zeros((part, width), F32)
                for t in range(2 * PT_DEV):
                    block = b_send[k, t] if t < PT_DEV else b_buf[k, t - PT_DEV]
                    total = total + picked(q, t, block)
                if o == 0:
                    ag_buf[k, 0, s] = total
                else:
                    ag_send[k, o - 1, s] = total
            if o > 0:
                ag_copy(k, o).start()

    def stage_row_project(layer):
        for o in range(1, np_):
            rr_copy(o).wait()
        total = row_send[b]
        for o in range(1, np_):
            total = total + row_rs[o - 1]
        term = (total * row_scale[...]).astype(BF16)
        row_ag_send[...] = (
            jnp.dot(term, wrow_ref[layer], preferred_element_type=F32) + bias_ref[layer])
        for o in range(1, np_):
            ra_copy(o).start()

    def stage_row_collect(layer):
        for o in range(1, np_):
            ra_copy(o).wait()

        def place(j, block):
            return block

        for j in range(np_):
            o = lax.rem(b - j + np_, np_)
            got = row_ag[jnp.maximum(o - 1, 0)]
            block = jnp.where(jnp.full(got.shape, o, jnp.int32) == 0, row_ag_send[...], got)
            at = j * share
            row_p[at // rows, at % rows:at % rows + share, :] = block

    def exchange(layer, carry):
        for wave in range(nk + 2):
            if wave < nk:
                stage_sum(layer, wave)
            if wave == nk - 1:
                stage_row_project(layer)
            if 0 <= wave - 1 < nk:
                stage_project(layer, wave - 1)
            if 0 <= wave - 2 < nk:
                stage_choose(layer, wave - 2)
        stage_row_collect(layer)
        for k in range(nk):
            for o in range(1, nv):
                ag_copy(k, o).wait()

            @pl.when(layer < layers - 1)
            def _():
                layer_chunk(layer, k)
                send_cols(k)

        @pl.when(layer < layers - 1)
        def _():
            send_rows()

        @pl.when(layer == layers - 2)
        def _():
            pltpu.make_async_copy(cur, cur_out, out_sem).start()
        return carry

    lax.fori_loop(0, layers, exchange, 0)
    for s in range(slots):
        rowp_out[s] = row_p[tiles_ref[s, 0]]
        for k in range(nk):
            for j in range(nv):
                at = k * chunk + j * part
                colp_out[s, at:at + part, :] = ag_buf[k, lax.rem(a - j + nv, nv), s]
    pltpu.make_async_copy(cur, cur_out, out_sem).wait()


def last_layer_kernel(cur_ref, mask_ref, w_ref, colp_ref, rowp_ref, out_ref):
    _, group, cols, width = cur_ref.shape
    x = cur_ref[0].reshape(group * cols, width)
    mt = mask_ref[0].astype(F32).T
    for i in range(group):
        z = jnp.dot(x[i * cols:(i + 1) * cols], w_ref[0], preferred_element_type=F32)
        y = z + colp_ref[0] + rowp_ref[0, i:i + 1, :]
        m = jnp.broadcast_to(mt[:, i:i + 1], (cols, width))
        out_ref[0, i] = (jnp.maximum(y, 0.0) * m).astype(BF16)


def shards(nv, np_, features, tiles, masks, w_self, w_col, w_row, bias):
    slots, rows, cols, width = features.shape
    layers = w_self.shape[0]
    nk = max(cols // (8 * nv), 1)
    chunk = cols // nk
    part = chunk // nv
    share = VT_DEV * rows // np_
    lanes = 128
    vmem = pltpu.VMEM
    dma = pltpu.SemaphoreType.DMA
    whole = pl.BlockSpec(memory_space=pltpu.VMEM)
    scratch = [
        vmem((slots, rows, cols, width), BF16),
        vmem((slots, cols, rows), F32),
        vmem((nk, nv, slots, part, width), F32),
        vmem((nk, nv - 1, slots, part, width), F32),
        vmem((nk, PT_DEV, part, width), F32),
        vmem((nk, PT_DEV, part, width), F32),
        vmem((nk, PT_DEV, part, width), F32),
        vmem((nk, PT_DEV, part, width), F32),
        vmem((nk, PT_DEV, part, width), F32),
        vmem((nk, nv - 1, slots, part, width), F32),
        vmem((nk, nv, slots, part, width), F32),
        vmem((slots, rows, width), F32),
        vmem((np_, share, width), F32),
        vmem((np_ - 1, share, width), F32),
        vmem((share, width), F32),
        vmem((np_ - 1, share, width), F32),
        vmem((VT_DEV, rows, width), F32),
        vmem((nv, slots, nk * part + 8, lanes), F32),
        vmem((nv - 1, slots, nk * part + 8, lanes), F32),
        vmem((PT_DEV, nk * part, lanes), F32),
        vmem((PT_DEV, nk * part, lanes), F32),
        vmem((np_, share, lanes), F32),
        vmem((np_ - 1, share, lanes), F32),
        vmem((PT_DEV, nk * part, lanes), F32),
        vmem((share, width), F32),
        vmem((nv, slots, 8, width), F32),
        dma((nk,)),
        dma,
        dma((nk, nv - 1)), dma((nk, nv - 1)),
        dma((nk,)), dma((nk,)), dma((nk,)), dma((nk,)),
        dma((nk, nv - 1)), dma((nk, nv - 1)),
        dma((np_ - 1,)), dma((np_ - 1,)), dma((np_ - 1,)), dma((np_ - 1,)),
        dma((nv - 1,)), dma((nv - 1,)),
        dma((1,)), dma((1,)),
        dma((np_ - 1,)), dma((np_ - 1,)),
    ]
    current, colp, rowp = pl.pallas_call(
        functools.partial(exchange_kernel, nv, np_, nk),
        out_shape=(
            jax.ShapeDtypeStruct(features.shape, BF16),
            jax.ShapeDtypeStruct((slots, cols, width), F32),
            jax.ShapeDtypeStruct((slots, rows, width), F32),
        ),
        in_specs=[
            pl.BlockSpec(memory_space=pltpu.SMEM),
            pl.BlockSpec(memory_space=pl.ANY),
            whole, whole, whole, whole, whole,
        ],
        out_specs=(pl.BlockSpec(memory_space=pl.ANY), whole, whole),
        scratch_shapes=scratch,
        compiler_params=pltpu.CompilerParams(
            collective_id=0, has_side_effects=True, vmem_limit_bytes=60 * 1024 * 1024),
        name="exchange",
    )(tiles, features, masks, w_self, w_col, w_row, bias.reshape(layers, 1, width))
    group = 8
    return pl.pallas_call(
        last_layer_kernel,
        grid=(slots, rows // group),
        out_shape=jax.ShapeDtypeStruct(features.shape, BF16),
        in_specs=[
            pl.BlockSpec((1, group, cols, width), lambda s, g: (s, g, 0, 0)),
            pl.BlockSpec((1, group, cols), lambda s, g: (s, g, 0)),
            pl.BlockSpec((1, width, width), lambda s, g: (layers - 1, 0, 0)),
            pl.BlockSpec((1, cols, width), lambda s, g: (s, 0, 0)),
            pl.BlockSpec((1, group, width), lambda s, g: (s, g, 0)),
        ],
        out_specs=pl.BlockSpec((1, group, cols, width), lambda s, g: (s, g, 0, 0)),
        name="last_layer",
    )(current, masks, w_self, colp, rowp)


def solution(mesh):
    in_specs = (
        P(("view", "point"), None, None, None),
        P(("view", "point"), None),
        P(("view", "point"), None, None),
        P(), P(), P(), P(),
    )
    out_specs = P(("view", "point"), None, None, None)
    body = functools.partial(shards, mesh.shape["view"], mesh.shape["point"])
    return jax.shard_map(body, mesh=mesh, in_specs=in_specs, out_specs=out_specs, check_vma=False)
```

```python
import functools

import jax
import jax.numpy as jnp
from jax import lax
from jax.experimental import pallas as pl
from jax.experimental.pallas import tpu as pltpu
from jax.sharding import PartitionSpec as P

VT_DEV = 4
PT_DEV = 4
MESH = pl.DeviceIdType.MESH
F32 = jnp.float32
BF16 = jnp.bfloat16


def wide(x, width):
    reps = width // x.shape[-1]
    return x if reps == 1 else jnp.concatenate([x] * reps, axis=-1)


def exchange_kernel(
    nv, np_, nk,
    tiles_ref, feat_ref, mask_ref, wself_ref, wcol_ref, wrow_ref, bias_ref,
    cur_out, colp_out, rowp_out,
    cur, pick, gather_mat, scatter_mat, col_send, rs_buf, f_send, f_buf, own_acc, b_send, b_buf, ag_send, ag_buf,
    row_acc, row_send, row_rs, row_ag_send, row_ag, row_p,
    ci_send, ci_buf, cf_send, cf_buf, ri_send, ri_buf, col_scale, row_scale, q_all,
    feat_sem, out_sem, rs_s, rs_r, f_s, f_r, b_s, b_r, ag_s, ag_r,
    rr_s, rr_r, ra_s, ra_r, ci_s, ci_r, cf_s, cf_r, ri_s, ri_r,
):
    a = lax.axis_index("view")
    b = lax.axis_index("point")
    slots, rows, cols, width = cur.shape
    layers = wself_ref.shape[0]
    chunk = cols // nk
    part = chunk // nv
    share = row_send.shape[1]
    nxt = lax.rem(b + 1, np_)
    prv = lax.rem(b + np_ - 1, np_)

    def remote(src, dst, ssem, rsem, va, pb):
        return pltpu.make_async_remote_copy(
            src_ref=src, dst_ref=dst, send_sem=ssem, recv_sem=rsem,
            device_id=(va, pb), device_id_type=MESH,
        )

    def view_at(o):
        return lax.rem(a + o, nv)

    def point_at(o):
        return lax.rem(b + o, np_)

    def rs_copy(k, o):
        return remote(col_send.at[k, view_at(o)], rs_buf.at[k, o - 1],
                      rs_s.at[k, o - 1], rs_r.at[k, o - 1], view_at(o), b)

    def ag_copy(k, o):
        return remote(ag_send.at[k, o - 1], ag_buf.at[k, o],
                      ag_s.at[k, o - 1], ag_r.at[k, o - 1], view_at(o), b)

    def f_copy(k):
        return remote(f_send.at[k], f_buf.at[k], f_s.at[k], f_r.at[k], a, nxt)

    def b_copy(k):
        return remote(b_send.at[k], b_buf.at[k], b_s.at[k], b_r.at[k], a, prv)

    def rr_copy(o):
        return remote(row_send.at[point_at(o)], row_rs.at[o - 1],
                      rr_s.at[o - 1], rr_r.at[o - 1], a, point_at(o))

    def ra_copy(o):
        return remote(row_ag_send, row_ag.at[o - 1], ra_s.at[o - 1], ra_r.at[o - 1], a, point_at(o))

    def ci_copy(o):
        return remote(ci_send.at[view_at(o)], ci_buf.at[o - 1],
                      ci_s.at[o - 1], ci_r.at[o - 1], view_at(o), b)

    def cf_copy():
        return remote(cf_send, cf_buf, cf_s.at[0], cf_r.at[0], a, nxt)

    def ri_copy(o):
        return remote(ri_send.at[point_at(o)], ri_buf.at[o - 1],
                      ri_s.at[o - 1], ri_r.at[o - 1], a, point_at(o))

    def feat_copy(k):
        span = pl.ds(k * chunk, chunk)
        return pltpu.make_async_copy(
            feat_ref.at[:, :, span, :], cur.at[:, :, span, :], feat_sem.at[k])

    for k in range(nk):
        feat_copy(k).start()

    barrier = pltpu.get_barrier_semaphore()
    for o in range(1, nv):
        pl.semaphore_signal(barrier, inc=1, device_id=(view_at(o), b), device_id_type=MESH)
    for o in range(1, np_):
        pl.semaphore_signal(barrier, inc=1, device_id=(a, point_at(o)), device_id_type=MESH)

    group = pick.shape[4] // chunk

    lanes = ci_send.shape[-1]
    per_part = nk * part
    for s in range(slots):
        m = mask_ref[s].astype(F32)
        ccount = jnp.broadcast_to(jnp.sum(m.T, axis=1, keepdims=True), (cols, lanes))
        q = jnp.full((8, lanes), tiles_ref[1, s], jnp.int32).astype(F32)
        for j in range(nv):
            for k in range(nk):
                at = k * chunk + j * part
                ci_send[j, s, k * part:(k + 1) * part, :] = ccount[at:at + part]
            ci_send[j, s, per_part:, :] = q
    for v in range(VT_DEV):
        total = jnp.zeros((rows, lanes), F32)
        for s in range(slots):
            rcount = jnp.broadcast_to(
                jnp.sum(mask_ref[s].astype(F32), axis=1, keepdims=True), (rows, lanes))
            hit = jnp.full((rows, lanes), tiles_ref[0, s], jnp.int32) == v
            total = total + jnp.where(hit, rcount, 0.0)
        for i in range(max(rows // share, 1)):
            at = v * rows + i * share
            ri_send[at // share] = total[i * share:(i + 1) * share]

    pl.semaphore_wait(barrier, nv - 1 + np_ - 1)
    for o in range(1, nv):
        ci_copy(o).start()
    for o in range(1, np_):
        ri_copy(o).start()

    def build_pick(s, carry):
        shape = (group, group * chunk)
        lane = lax.broadcasted_iota(jnp.int32, shape, 1)
        of_view = lane // chunk == lax.broadcasted_iota(jnp.int32, shape, 0)
        shape = (chunk, group * chunk)
        lane = lax.broadcasted_iota(jnp.int32, shape, 1)
        of_point = lane % chunk == lax.broadcasted_iota(jnp.int32, shape, 0)
        for g in range(rows // group):
            m = mask_ref[s, g * group:(g + 1) * group, :].astype(F32)
            for k in range(nk):
                tiled = jnp.concatenate([m[:, k * chunk:(k + 1) * chunk]] * group, axis=1)
                by_view = jnp.where(of_view, tiled, 0.0)
                flat = jnp.sum(by_view, axis=0, keepdims=True)
                by_point = jnp.where(of_point, jnp.broadcast_to(flat, shape), 0.0)
                both = jnp.concatenate([by_point, by_view, jnp.zeros_like(by_view)], axis=0)
                pick[s, k, g] = both.astype(BF16)
        return carry

    lax.fori_loop(0, slots, build_pick, 0)

    def sum_rows(k, s, value_of):
        col = jnp.zeros((chunk, width), F32)
        for g in range(rows // group):
            both = jnp.dot(pick[s, k, g], value_of(g), preferred_element_type=F32)
            col = col + both[:chunk]
            new = both[chunk:chunk + group]
            at = pl.ds(g * group, group)
            if k == 0:
                row_acc[s, at, :] = new
            else:
                row_acc[s, at, :] = row_acc[s, at, :] + new
        for j in range(nv):
            col_send[k, j, s] = col[j * part:(j + 1) * part]

    def entries(k, s, g):
        span = pl.ds(k * chunk, chunk)
        return cur[s, g * group:(g + 1) * group, span, :].reshape(group * chunk, width)

    def first_sums(k):
        def slot(s, carry):
            sum_rows(k, s, lambda g: entries(k, s, g))
            return carry
        lax.fori_loop(0, slots, slot, 0)

    def layer_chunk(layer, k):
        span = pl.ds(k * chunk, chunk)

        def slot(s, carry):
            colp = jnp.concatenate(
                [ag_buf[k, lax.rem(a - j + nv, nv), s] for j in range(nv)], axis=0)
            v = tiles_ref[0, s]
            rowp = row_p[v]

            def value_of(g):
                z = jnp.dot(entries(k, s, g), wself_ref[layer], preferred_element_type=F32)
                z = z.reshape(group, chunk, width)
                y = z + colp[None] + rowp[g * group:(g + 1) * group][:, None, :]
                y = jnp.maximum(y, 0.0).astype(BF16)
                cur[s, g * group:(g + 1) * group, span, :] = y
                return y.reshape(group * chunk, width)
            sum_rows(k, s, value_of)
            return carry
        lax.fori_loop(0, slots, slot, 0)

    def send_rows():
        for v in range(VT_DEV):
            total = jnp.zeros((rows, width), F32)
            for s in range(slots):
                hit = jnp.full((rows, width), tiles_ref[0, s], jnp.int32) == v
                total = total + jnp.where(hit, row_acc[s], 0.0)
            for i in range(max(rows // share, 1)):
                at = v * rows + i * share
                row_send[at // share] = total[i * share:(i + 1) * share]
        for o in range(1, np_):
            rr_copy(o).start()

    def send_cols(k):
        for o in range(1, nv):
            rs_copy(k, o).start()

    def halves(x):
        high = x.astype(BF16)
        return jnp.concatenate([high, (x - high.astype(F32)).astype(BF16)], axis=0)

    def picked(q, t, block):
        return jnp.where(q == float(t), block, 0.0)

    for k in range(nk):
        feat_copy(k).wait()
        first_sums(k)
        send_cols(k)
    send_rows()

    for o in range(1, nv):
        ci_copy(o).wait()
    for s in range(slots):
        q_all[0, s] = wide(ci_send[a, s, per_part:, :], width)
        for o in range(1, nv):
            q_all[o, s] = wide(ci_buf[o - 1, s, per_part:, :], width)
    shape = scatter_mat.shape
    lane = lax.broadcasted_iota(jnp.int32, (8, shape[1]), 1) % (nv * slots * part)
    q_lane = jnp.zeros((8, shape[1]), F32)
    for o in range(nv):
        for s in range(slots):
            q = wide(ci_send[a, s, per_part:, :] if o == 0 else ci_buf[o - 1, s, per_part:, :],
                     shape[1])
            q_lane = jnp.where(lane // part == o * slots + s, q, q_lane)
    row = lax.broadcasted_iota(jnp.int32, shape, 0)
    lane = lax.broadcasted_iota(jnp.int32, shape, 1)
    q_lane = jnp.concatenate([q_lane] * (shape[0] // 8), axis=0)
    hit = (q_lane == (row // part).astype(F32)) & (row % part == lane % part)
    scatter_mat[...] = jnp.where(hit, 1.0, 0.0).astype(BF16)
    shape = (part, gather_mat.shape[1])
    lane = lax.broadcasted_iota(jnp.int32, shape, 1)
    same = lane % part == lax.broadcasted_iota(jnp.int32, shape, 0) % part
    tile = ((lane // part) % (2 * PT_DEV)).astype(F32)
    for o in range(nv):
        for s in range(slots):
            q = jnp.concatenate([q_all[(nv - o) % nv, s]] * (part // 8), axis=0)
            hit = (q[:, :shape[1]] == tile) & same
            at = (o * slots + s) * part
            gather_mat[at:at + part, :] = jnp.where(hit, 1.0, 0.0)
    for t in range(2 * PT_DEV):
        total = jnp.zeros((per_part, lanes), F32)
        for s in range(slots):
            for o in range(nv):
                block = ci_send.at[a] if o == 0 else ci_buf.at[o - 1]
                q = jnp.concatenate([block[s, per_part:, :]] * (per_part // 8), axis=0)
                total = total + picked(q, t, block[s, :per_part, :])
        if t < PT_DEV:
            col_scale[t] = total
        else:
            cf_send[t - PT_DEV] = total
    cf_copy().start()
    for o in range(1, np_):
        ri_copy(o).wait()
    total = ri_send[b]
    for o in range(1, np_):
        total = total + ri_buf[o - 1]
    row_scale[...] = wide(1.0 / jnp.sqrt(jnp.maximum(total, 1.0)), width)
    cf_copy().wait()
    for t in range(PT_DEV):
        total = col_scale[t] + cf_buf[t]
        col_scale[t] = 1.0 / jnp.sqrt(jnp.maximum(total, 1.0))

    def stage_sum(layer, k):
        for o in range(1, nv):
            rs_copy(k, o).wait()
        blocks = [col_send[k, a] if o == 0 else rs_buf[k, o - 1] for o in range(nv)]
        blocks = jnp.concatenate([x.reshape(slots * part, width) for x in blocks], axis=0)
        total = jnp.dot(scatter_mat[...], halves(blocks), preferred_element_type=F32)
        total = total.reshape(2 * PT_DEV, part, width)
        own_acc[k] = total[:PT_DEV]
        f_send[k] = total[PT_DEV:]
        f_copy(k).start()

    def stage_project(layer, k):
        f_copy(k).wait()
        scale = wide(col_scale[:, k * part:(k + 1) * part, :], width)
        term = ((own_acc[k] + f_buf[k]) * scale).reshape(PT_DEV * part, width).astype(BF16)
        out = jnp.dot(term, wcol_ref[layer], preferred_element_type=F32)
        b_send[k] = out.reshape(PT_DEV, part, width)
        b_copy(k).start()

    def stage_choose(layer, k):
        b_copy(k).wait()
        blocks = jnp.concatenate([b_send[k], b_buf[k]], axis=0)
        blocks = halves(blocks.reshape(2 * PT_DEV * part, width))
        chosen = jnp.dot(gather_mat[...].astype(BF16), blocks, preferred_element_type=F32)
        chosen = chosen.reshape(nv, slots, part, width)
        ag_buf[k, 0] = chosen[0]
        for o in range(1, nv):
            ag_send[k, o - 1] = chosen[o]
            ag_copy(k, o).start()

    def stage_row_project(layer):
        for o in range(1, np_):
            rr_copy(o).wait()
        total = row_send[b]
        for o in range(1, np_):
            total = total + row_rs[o - 1]
        term = (total * row_scale[...]).astype(BF16)
        row_ag_send[...] = (
            jnp.dot(term, wrow_ref[layer], preferred_element_type=F32)
            + bias_ref[pl.ds(layer, 1), :])
        for o in range(1, np_):
            ra_copy(o).start()

    def stage_row_collect(layer):
        for o in range(1, np_):
            ra_copy(o).wait()

        for j in range(np_):
            o = lax.rem(b - j + np_, np_)
            got = row_ag[jnp.maximum(o - 1, 0)]
            block = jnp.where(jnp.full(got.shape, o, jnp.int32) == 0, row_ag_send[...], got)
            at = j * share
            row_p[at // rows, at % rows:at % rows + share, :] = block

    def exchange(layer, carry):
        for wave in range(nk + 2):
            if wave < nk:
                stage_sum(layer, wave)
            if wave == nk - 1:
                stage_row_project(layer)
            if 0 <= wave - 1 < nk:
                stage_project(layer, wave - 1)
            if 0 <= wave - 2 < nk:
                stage_choose(layer, wave - 2)
        stage_row_collect(layer)
        for k in range(nk):
            for o in range(1, nv):
                ag_copy(k, o).wait()

            @pl.when(layer < layers - 1)
            def _():
                layer_chunk(layer, k)
                send_cols(k)

        @pl.when(layer < layers - 1)
        def _():
            send_rows()

        @pl.when(layer == layers - 2)
        def _():
            pltpu.make_async_copy(cur, cur_out, out_sem).start()
        return carry

    lax.fori_loop(0, layers, exchange, 0)
    for s in range(slots):
        rowp_out[s] = row_p[tiles_ref[0, s]]
        for k in range(nk):
            for j in range(nv):
                at = k * chunk + j * part
                colp_out[s, at:at + part, :] = ag_buf[k, lax.rem(a - j + nv, nv), s]
    pltpu.make_async_copy(cur, cur_out, out_sem).wait()


def last_layer_kernel(cur_ref, mask_ref, w_ref, colp_ref, rowp_ref, out_ref):
    _, group, cols, width = cur_ref.shape
    x = cur_ref[0].reshape(group * cols, width)
    mt = mask_ref[0].astype(F32).T
    for i in range(0, group, 2):
        z = jnp.dot(x[i * cols:(i + 2) * cols], w_ref[0], preferred_element_type=F32)
        for h in range(2):
            y = z[h * cols:(h + 1) * cols] + colp_ref[0] + rowp_ref[0, i + h:i + h + 1, :]
            m = jnp.broadcast_to(mt[:, i + h:i + h + 1], (cols, width))
            out_ref[0, i + h] = (jnp.maximum(y, 0.0) * m).astype(BF16)


def shards(nv, np_, features, tiles, masks, w_self, w_col, w_row, bias):
    slots, rows, cols, width = features.shape
    layers = w_self.shape[0]
    nk = max(cols // (8 * nv), 1)
    chunk = cols // nk
    part = chunk // nv
    share = VT_DEV * rows // np_
    lanes = 128
    group = 256 // chunk
    vmem = pltpu.VMEM
    dma = pltpu.SemaphoreType.DMA
    whole = pl.BlockSpec(memory_space=pltpu.VMEM)
    scratch = [
        vmem((slots, rows, cols, width), BF16),
        vmem((slots, nk, rows // group, chunk + 2 * group, group * chunk), BF16),
        vmem((nv * slots * part, 4 * PT_DEV * part), F32),
        vmem((2 * PT_DEV * part, 2 * nv * slots * part), BF16),
        vmem((nk, nv, slots, part, width), F32),
        vmem((nk, nv - 1, slots, part, width), F32),
        vmem((nk, PT_DEV, part, width), F32),
        vmem((nk, PT_DEV, part, width), F32),
        vmem((nk, PT_DEV, part, width), F32),
        vmem((nk, PT_DEV, part, width), F32),
        vmem((nk, PT_DEV, part, width), F32),
        vmem((nk, nv - 1, slots, part, width), F32),
        vmem((nk, nv, slots, part, width), F32),
        vmem((slots, rows, width), F32),
        vmem((np_, share, width), F32),
        vmem((np_ - 1, share, width), F32),
        vmem((share, width), F32),
        vmem((np_ - 1, share, width), F32),
        vmem((VT_DEV, rows, width), F32),
        vmem((nv, slots, nk * part + 8, lanes), F32),
        vmem((nv - 1, slots, nk * part + 8, lanes), F32),
        vmem((PT_DEV, nk * part, lanes), F32),
        vmem((PT_DEV, nk * part, lanes), F32),
        vmem((np_, share, lanes), F32),
        vmem((np_ - 1, share, lanes), F32),
        vmem((PT_DEV, nk * part, lanes), F32),
        vmem((share, width), F32),
        vmem((nv, slots, 8, width), F32),
        dma((nk,)),
        dma,
        dma((nk, nv - 1)), dma((nk, nv - 1)),
        dma((nk,)), dma((nk,)), dma((nk,)), dma((nk,)),
        dma((nk, nv - 1)), dma((nk, nv - 1)),
        dma((np_ - 1,)), dma((np_ - 1,)), dma((np_ - 1,)), dma((np_ - 1,)),
        dma((nv - 1,)), dma((nv - 1,)),
        dma((1,)), dma((1,)),
        dma((np_ - 1,)), dma((np_ - 1,)),
    ]
    current, colp, rowp = pl.pallas_call(
        functools.partial(exchange_kernel, nv, np_, nk),
        out_shape=(
            jax.ShapeDtypeStruct(features.shape, BF16),
            jax.ShapeDtypeStruct((slots, cols, width), F32),
            jax.ShapeDtypeStruct((slots, rows, width), F32),
        ),
        in_specs=[
            pl.BlockSpec(memory_space=pltpu.SMEM),
            pl.BlockSpec(memory_space=pl.ANY),
            whole, whole, whole, whole, whole,
        ],
        out_specs=(pl.BlockSpec(memory_space=pl.ANY), whole, whole),
        scratch_shapes=scratch,
        compiler_params=pltpu.CompilerParams(
            collective_id=0, has_side_effects=True, vmem_limit_bytes=60 * 1024 * 1024),
        name="exchange",
    )(tiles.T, features, masks, w_self, w_col, w_row, bias)
    group = 16
    return pl.pallas_call(
        last_layer_kernel,
        grid=(slots, rows // group),
        out_shape=jax.ShapeDtypeStruct(features.shape, BF16),
        in_specs=[
            pl.BlockSpec((1, group, cols, width), lambda s, g: (s, g, 0, 0)),
            pl.BlockSpec((1, group, cols), lambda s, g: (s, g, 0)),
            pl.BlockSpec((1, width, width), lambda s, g: (layers - 1, 0, 0)),
            pl.BlockSpec((1, cols, width), lambda s, g: (s, 0, 0)),
            pl.BlockSpec((1, group, width), lambda s, g: (s, g, 0)),
        ],
        out_specs=pl.BlockSpec((1, group, cols, width), lambda s, g: (s, g, 0, 0)),
        name="last_layer",
    )(current, masks, w_self, colp, rowp)


def solution(mesh):
    in_specs = (
        P(("view", "point"), None, None, None),
        P(("view", "point"), None),
        P(("view", "point"), None, None),
        P(), P(), P(), P(),
    )
    out_specs = P(("view", "point"), None, None, None)
    body = functools.partial(shards, mesh.shape["view"], mesh.shape["point"])
    return jax.shard_map(body, mesh=mesh, in_specs=in_specs, out_specs=out_specs, check_vma=False)
```

```python
import functools

import jax
import jax.numpy as jnp
from jax import lax
from jax.experimental import pallas as pl
from jax.experimental.pallas import tpu as pltpu
from jax.sharding import PartitionSpec as P

VT_DEV = 4
PT_DEV = 4
MESH = pl.DeviceIdType.MESH
F32 = jnp.float32
BF16 = jnp.bfloat16


def wide(x, width):
    reps = width // x.shape[-1]
    return x if reps == 1 else jnp.concatenate([x] * reps, axis=-1)


def exchange_kernel(
    nv, np_, nk,
    tiles_ref, feat_ref, mask_ref, wself_ref, wcol_ref, wrow_ref, bias_ref,
    cur_out, colp_out, rowp_out,
    cur, pick, gather_mat, scatter_mat, col_send, rs_buf, f_send, f_buf, own_acc, b_send, b_buf, ag_send, ag_buf,
    row_acc, row_send, row_rs, row_ag_send, row_ag, row_p,
    ci_send, ci_buf, cf_send, cf_buf, ri_send, ri_buf, col_scale, row_scale, q_all,
    feat_sem, out_sem, rs_s, rs_r, f_s, f_r, b_s, b_r, ag_s, ag_r,
    rr_s, rr_r, ra_s, ra_r, ci_s, ci_r, cf_s, cf_r, ri_s, ri_r,
):
    a = lax.axis_index("view")
    b = lax.axis_index("point")
    slots, rows, cols, width = cur.shape
    layers = wself_ref.shape[0]
    chunk = cols // nk
    part = chunk // nv
    share = row_send.shape[1]
    nxt = lax.rem(b + 1, np_)
    prv = lax.rem(b + np_ - 1, np_)

    def remote(src, dst, ssem, rsem, va, pb):
        return pltpu.make_async_remote_copy(
            src_ref=src, dst_ref=dst, send_sem=ssem, recv_sem=rsem,
            device_id=(va, pb), device_id_type=MESH,
        )

    def view_at(o):
        return lax.rem(a + o, nv)

    def point_at(o):
        return lax.rem(b + o, np_)

    def rs_copy(k, o):
        return remote(col_send.at[k, view_at(o)], rs_buf.at[k, o - 1],
                      rs_s.at[k, o - 1], rs_r.at[k, o - 1], view_at(o), b)

    def ag_copy(k, o):
        return remote(ag_send.at[k, o - 1], ag_buf.at[k, o],
                      ag_s.at[k, o - 1], ag_r.at[k, o - 1], view_at(o), b)

    def f_copy(k):
        return remote(f_send.at[k], f_buf.at[k], f_s.at[k], f_r.at[k], a, nxt)

    def b_copy(k):
        return remote(b_send.at[k], b_buf.at[k], b_s.at[k], b_r.at[k], a, prv)

    def rr_copy(o):
        return remote(row_send.at[point_at(o)], row_rs.at[o - 1],
                      rr_s.at[o - 1], rr_r.at[o - 1], a, point_at(o))

    def ra_copy(o):
        return remote(row_ag_send, row_ag.at[o - 1], ra_s.at[o - 1], ra_r.at[o - 1], a, point_at(o))

    def ci_copy(o):
        return remote(ci_send.at[view_at(o)], ci_buf.at[o - 1],
                      ci_s.at[o - 1], ci_r.at[o - 1], view_at(o), b)

    def cf_copy():
        return remote(cf_send, cf_buf, cf_s.at[0], cf_r.at[0], a, nxt)

    def ri_copy(o):
        return remote(ri_send.at[point_at(o)], ri_buf.at[o - 1],
                      ri_s.at[o - 1], ri_r.at[o - 1], a, point_at(o))

    def feat_copy(k):
        span = pl.ds(k * chunk, chunk)
        return pltpu.make_async_copy(
            feat_ref.at[:, :, span, :], cur.at[:, :, span, :], feat_sem.at[k])

    for k in range(nk):
        feat_copy(k).start()

    barrier = pltpu.get_barrier_semaphore()
    for o in range(1, nv):
        pl.semaphore_signal(barrier, inc=1, device_id=(view_at(o), b), device_id_type=MESH)
    for o in range(1, np_):
        pl.semaphore_signal(barrier, inc=1, device_id=(a, point_at(o)), device_id_type=MESH)

    group = pick.shape[4] // chunk

    lanes = ci_send.shape[-1]
    per_part = nk * part
    for s in range(slots):
        m = mask_ref[s].astype(F32)
        ccount = jnp.broadcast_to(jnp.sum(m.T, axis=1, keepdims=True), (cols, lanes))
        q = jnp.full((8, lanes), tiles_ref[1, s], jnp.int32).astype(F32)
        for j in range(nv):
            for k in range(nk):
                at = k * chunk + j * part
                ci_send[j, s, k * part:(k + 1) * part, :] = ccount[at:at + part]
            ci_send[j, s, per_part:, :] = q
    for v in range(VT_DEV):
        total = jnp.zeros((rows, lanes), F32)
        for s in range(slots):
            rcount = jnp.broadcast_to(
                jnp.sum(mask_ref[s].astype(F32), axis=1, keepdims=True), (rows, lanes))
            hit = jnp.full((rows, lanes), tiles_ref[0, s], jnp.int32) == v
            total = total + jnp.where(hit, rcount, 0.0)
        for i in range(max(rows // share, 1)):
            at = v * rows + i * share
            ri_send[at // share] = total[i * share:(i + 1) * share]

    pl.semaphore_wait(barrier, nv - 1 + np_ - 1)
    for o in range(1, nv):
        ci_copy(o).start()
    for o in range(1, np_):
        ri_copy(o).start()

    def build_pick(s, carry):
        shape = (group, group * chunk)
        lane = lax.broadcasted_iota(jnp.int32, shape, 1)
        of_view = lane // chunk == lax.broadcasted_iota(jnp.int32, shape, 0)
        shape = (chunk, group * chunk)
        lane = lax.broadcasted_iota(jnp.int32, shape, 1)
        of_point = lane % chunk == lax.broadcasted_iota(jnp.int32, shape, 0)
        for g in range(rows // group):
            m = mask_ref[s, g * group:(g + 1) * group, :].astype(F32)
            for k in range(nk):
                tiled = jnp.concatenate([m[:, k * chunk:(k + 1) * chunk]] * group, axis=1)
                by_view = jnp.where(of_view, tiled, 0.0)
                flat = jnp.sum(by_view, axis=0, keepdims=True)
                by_point = jnp.where(of_point, jnp.broadcast_to(flat, shape), 0.0)
                both = jnp.concatenate([by_point, by_view, jnp.zeros_like(by_view)], axis=0)
                pick[s, k, g] = both.astype(BF16)
        return carry

    lax.fori_loop(0, slots, build_pick, 0)

    def sum_rows(k, s, value_of):
        col = jnp.zeros((chunk, width), F32)
        for g in range(rows // group):
            both = jnp.dot(pick[s, k, g], value_of(g), preferred_element_type=F32)
            col = col + both[:chunk]
            new = both[chunk:chunk + group]
            at = pl.ds(g * group, group)
            if k == 0:
                row_acc[s, at, :] = new
            else:
                row_acc[s, at, :] = row_acc[s, at, :] + new
        for j in range(nv):
            col_send[k, j, s] = col[j * part:(j + 1) * part]

    def entries(k, s, g):
        span = pl.ds(k * chunk, chunk)
        return cur[s, g * group:(g + 1) * group, span, :].reshape(group * chunk, width)

    def first_sums(k):
        def slot(s, carry):
            sum_rows(k, s, lambda g: entries(k, s, g))
            return carry
        lax.fori_loop(0, slots, slot, 0, unroll=2 if slots % 2 == 0 else 1)

    def layer_chunk(layer, k):
        span = pl.ds(k * chunk, chunk)

        def slot(s, carry):
            colp = jnp.concatenate(
                [ag_buf[k, lax.rem(a - j + nv, nv), s] for j in range(nv)], axis=0)
            v = tiles_ref[0, s]
            rowp = row_p[v]

            def value_of(g):
                z = jnp.dot(entries(k, s, g), wself_ref[layer], preferred_element_type=F32)
                z = z.reshape(group, chunk, width)
                y = z + colp[None] + rowp[g * group:(g + 1) * group][:, None, :]
                y = jnp.maximum(y, 0.0).astype(BF16)
                cur[s, g * group:(g + 1) * group, span, :] = y
                return y.reshape(group * chunk, width)
            sum_rows(k, s, value_of)
            return carry
        lax.fori_loop(0, slots, slot, 0, unroll=2 if slots % 2 == 0 else 1)

    def send_rows():
        for v in range(VT_DEV):
            total = jnp.zeros((rows, width), F32)
            for s in range(slots):
                hit = jnp.full((rows, width), tiles_ref[0, s], jnp.int32) == v
                total = total + jnp.where(hit, row_acc[s], 0.0)
            for i in range(max(rows // share, 1)):
                at = v * rows + i * share
                row_send[at // share] = total[i * share:(i + 1) * share]
        for o in range(1, np_):
            rr_copy(o).start()

    def send_cols(k):
        for o in range(1, nv):
            rs_copy(k, o).start()

    def halves(x):
        high = x.astype(BF16)
        return jnp.concatenate([high, (x - high.astype(F32)).astype(BF16)], axis=0)

    def picked(q, t, block):
        return jnp.where(q == float(t), block, 0.0)

    for k in range(nk):
        feat_copy(k).wait()
        first_sums(k)
        send_cols(k)
    send_rows()

    for o in range(1, nv):
        ci_copy(o).wait()
    for s in range(slots):
        q_all[0, s] = wide(ci_send[a, s, per_part:, :], width)
        for o in range(1, nv):
            q_all[o, s] = wide(ci_buf[o - 1, s, per_part:, :], width)
    shape = scatter_mat.shape
    lane = lax.broadcasted_iota(jnp.int32, (8, shape[1]), 1) % (nv * slots * part)
    q_lane = jnp.zeros((8, shape[1]), F32)
    for o in range(nv):
        for s in range(slots):
            q = wide(ci_send[a, s, per_part:, :] if o == 0 else ci_buf[o - 1, s, per_part:, :],
                     shape[1])
            q_lane = jnp.where(lane // part == o * slots + s, q, q_lane)
    row = lax.broadcasted_iota(jnp.int32, shape, 0)
    lane = lax.broadcasted_iota(jnp.int32, shape, 1)
    q_lane = jnp.concatenate([q_lane] * (shape[0] // 8), axis=0)
    hit = (q_lane == (row // part).astype(F32)) & (row % part == lane % part)
    scatter_mat[...] = jnp.where(hit, 1.0, 0.0).astype(BF16)
    shape = (part, gather_mat.shape[1])
    lane = lax.broadcasted_iota(jnp.int32, shape, 1)
    same = lane % part == lax.broadcasted_iota(jnp.int32, shape, 0) % part
    tile = ((lane // part) % (2 * PT_DEV)).astype(F32)
    for o in range(nv):
        for s in range(slots):
            q = jnp.concatenate([q_all[(nv - o) % nv, s]] * (part // 8), axis=0)
            hit = (q[:, :shape[1]] == tile) & same
            at = (o * slots + s) * part
            gather_mat[at:at + part, :] = jnp.where(hit, 1.0, 0.0)
    for t in range(2 * PT_DEV):
        total = jnp.zeros((per_part, lanes), F32)
        for s in range(slots):
            for o in range(nv):
                block = ci_send.at[a] if o == 0 else ci_buf.at[o - 1]
                q = jnp.concatenate([block[s, per_part:, :]] * (per_part // 8), axis=0)
                total = total + picked(q, t, block[s, :per_part, :])
        if t < PT_DEV:
            col_scale[t] = total
        else:
            cf_send[t - PT_DEV] = total
    cf_copy().start()
    for o in range(1, np_):
        ri_copy(o).wait()
    total = ri_send[b]
    for o in range(1, np_):
        total = total + ri_buf[o - 1]
    row_scale[...] = wide(1.0 / jnp.sqrt(jnp.maximum(total, 1.0)), width)
    cf_copy().wait()
    for t in range(PT_DEV):
        total = col_scale[t] + cf_buf[t]
        col_scale[t] = 1.0 / jnp.sqrt(jnp.maximum(total, 1.0))

    def stage_sum(layer, k):
        for o in range(1, nv):
            rs_copy(k, o).wait()
        blocks = [col_send[k, a] if o == 0 else rs_buf[k, o - 1] for o in range(nv)]
        blocks = jnp.concatenate([x.reshape(slots * part, width) for x in blocks], axis=0)
        total = jnp.dot(scatter_mat[...], halves(blocks), preferred_element_type=F32)
        total = total.reshape(2 * PT_DEV, part, width)
        own_acc[k] = total[:PT_DEV]
        f_send[k] = total[PT_DEV:]
        f_copy(k).start()

    def stage_project(layer, k):
        f_copy(k).wait()
        scale = wide(col_scale[:, k * part:(k + 1) * part, :], width)
        term = ((own_acc[k] + f_buf[k]) * scale).reshape(PT_DEV * part, width).astype(BF16)
        out = jnp.dot(term, wcol_ref[layer], preferred_element_type=F32)
        b_send[k] = out.reshape(PT_DEV, part, width)
        b_copy(k).start()

    def stage_choose(layer, k):
        b_copy(k).wait()
        blocks = jnp.concatenate([b_send[k], b_buf[k]], axis=0)
        blocks = halves(blocks.reshape(2 * PT_DEV * part, width))
        chosen = jnp.dot(gather_mat[...].astype(BF16), blocks, preferred_element_type=F32)
        chosen = chosen.reshape(nv, slots, part, width)
        ag_buf[k, 0] = chosen[0]
        for o in range(1, nv):
            ag_send[k, o - 1] = chosen[o]
            ag_copy(k, o).start()

    def stage_row_project(layer):
        for o in range(1, np_):
            rr_copy(o).wait()
        total = row_send[b]
        for o in range(1, np_):
            total = total + row_rs[o - 1]
        term = (total * row_scale[...]).astype(BF16)
        row_ag_send[...] = (
            jnp.dot(term, wrow_ref[layer], preferred_element_type=F32)
            + bias_ref[pl.ds(layer, 1), :])
        for o in range(1, np_):
            ra_copy(o).start()

    def stage_row_collect(layer):
        for o in range(1, np_):
            ra_copy(o).wait()

        for j in range(np_):
            o = lax.rem(b - j + np_, np_)
            got = row_ag[jnp.maximum(o - 1, 0)]
            block = jnp.where(jnp.full(got.shape, o, jnp.int32) == 0, row_ag_send[...], got)
            at = j * share
            row_p[at // rows, at % rows:at % rows + share, :] = block

    def exchange(layer, carry):
        for wave in range(nk + 2):
            if wave < nk:
                stage_sum(layer, wave)
            if 0 <= wave - 1 < nk:
                stage_project(layer, wave - 1)
            if 0 <= wave - 2 < nk:
                stage_choose(layer, wave - 2)
            if wave == nk - 1:
                stage_row_project(layer)
        stage_row_collect(layer)
        for k in range(nk):
            for o in range(1, nv):
                ag_copy(k, o).wait()

            @pl.when(layer < layers - 1)
            def _():
                layer_chunk(layer, k)
                send_cols(k)

        @pl.when(layer < layers - 1)
        def _():
            send_rows()

        @pl.when(layer == layers - 2)
        def _():
            pltpu.make_async_copy(cur, cur_out, out_sem).start()
        return carry

    lax.fori_loop(0, layers, exchange, 0)
    for s in range(slots):
        rowp_out[s] = row_p[tiles_ref[0, s]]
        for k in range(nk):
            for j in range(nv):
                at = k * chunk + j * part
                colp_out[s, at:at + part, :] = ag_buf[k, lax.rem(a - j + nv, nv), s]
    pltpu.make_async_copy(cur, cur_out, out_sem).wait()


def last_layer_kernel(cur_ref, mask_ref, w_ref, colp_ref, rowp_ref, out_ref):
    _, group, cols, width = cur_ref.shape
    x = cur_ref[0].reshape(group * cols, width)
    mt = mask_ref[0].astype(F32).T
    for i in range(0, group, 2):
        z = jnp.dot(x[i * cols:(i + 2) * cols], w_ref[0], preferred_element_type=F32)
        for h in range(2):
            y = z[h * cols:(h + 1) * cols] + colp_ref[0] + rowp_ref[0, i + h:i + h + 1, :]
            m = jnp.broadcast_to(mt[:, i + h:i + h + 1], (cols, width))
            out_ref[0, i + h] = (jnp.maximum(y, 0.0) * m).astype(BF16)


def shards(nv, np_, features, tiles, masks, w_self, w_col, w_row, bias):
    slots, rows, cols, width = features.shape
    layers = w_self.shape[0]
    nk = max(cols // (8 * nv), 1)
    chunk = cols // nk
    part = chunk // nv
    share = VT_DEV * rows // np_
    lanes = 128
    group = 256 // chunk
    vmem = pltpu.VMEM
    dma = pltpu.SemaphoreType.DMA
    whole = pl.BlockSpec(memory_space=pltpu.VMEM)
    scratch = [
        vmem((slots, rows, cols, width), BF16),
        vmem((slots, nk, rows // group, chunk + 2 * group, group * chunk), BF16),
        vmem((nv * slots * part, 4 * PT_DEV * part), F32),
        vmem((2 * PT_DEV * part, 2 * nv * slots * part), BF16),
        vmem((nk, nv, slots, part, width), F32),
        vmem((nk, nv - 1, slots, part, width), F32),
        vmem((nk, PT_DEV, part, width), F32),
        vmem((nk, PT_DEV, part, width), F32),
        vmem((nk, PT_DEV, part, width), F32),
        vmem((nk, PT_DEV, part, width), F32),
        vmem((nk, PT_DEV, part, width), F32),
        vmem((nk, nv - 1, slots, part, width), F32),
        vmem((nk, nv, slots, part, width), F32),
        vmem((slots, rows, width), F32),
        vmem((np_, share, width), F32),
        vmem((np_ - 1, share, width), F32),
        vmem((share, width), F32),
        vmem((np_ - 1, share, width), F32),
        vmem((VT_DEV, rows, width), F32),
        vmem((nv, slots, nk * part + 8, lanes), F32),
        vmem((nv - 1, slots, nk * part + 8, lanes), F32),
        vmem((PT_DEV, nk * part, lanes), F32),
        vmem((PT_DEV, nk * part, lanes), F32),
        vmem((np_, share, lanes), F32),
        vmem((np_ - 1, share, lanes), F32),
        vmem((PT_DEV, nk * part, lanes), F32),
        vmem((share, width), F32),
        vmem((nv, slots, 8, width), F32),
        dma((nk,)),
        dma,
        dma((nk, nv - 1)), dma((nk, nv - 1)),
        dma((nk,)), dma((nk,)), dma((nk,)), dma((nk,)),
        dma((nk, nv - 1)), dma((nk, nv - 1)),
        dma((np_ - 1,)), dma((np_ - 1,)), dma((np_ - 1,)), dma((np_ - 1,)),
        dma((nv - 1,)), dma((nv - 1,)),
        dma((1,)), dma((1,)),
        dma((np_ - 1,)), dma((np_ - 1,)),
    ]
    current, colp, rowp = pl.pallas_call(
        functools.partial(exchange_kernel, nv, np_, nk),
        out_shape=(
            jax.ShapeDtypeStruct(features.shape, BF16),
            jax.ShapeDtypeStruct((slots, cols, width), F32),
            jax.ShapeDtypeStruct((slots, rows, width), F32),
        ),
        in_specs=[
            pl.BlockSpec(memory_space=pltpu.SMEM),
            pl.BlockSpec(memory_space=pl.ANY),
            whole, whole, whole, whole, whole,
        ],
        out_specs=(pl.BlockSpec(memory_space=pl.ANY), whole, whole),
        scratch_shapes=scratch,
        compiler_params=pltpu.CompilerParams(
            collective_id=0, has_side_effects=True, vmem_limit_bytes=60 * 1024 * 1024),
        name="exchange",
    )(tiles.T, features, masks, w_self, w_col, w_row, bias)
    group = rows
    return pl.pallas_call(
        last_layer_kernel,
        grid=(slots, rows // group),
        out_shape=jax.ShapeDtypeStruct(features.shape, BF16),
        in_specs=[
            pl.BlockSpec((1, group, cols, width), lambda s, g: (s, g, 0, 0)),
            pl.BlockSpec((1, group, cols), lambda s, g: (s, g, 0)),
            pl.BlockSpec((1, width, width), lambda s, g: (layers - 1, 0, 0)),
            pl.BlockSpec((1, cols, width), lambda s, g: (s, 0, 0)),
            pl.BlockSpec((1, group, width), lambda s, g: (s, g, 0)),
        ],
        out_specs=pl.BlockSpec((1, group, cols, width), lambda s, g: (s, g, 0, 0)),
        name="last_layer",
    )(current, masks, w_self, colp, rowp)


def solution(mesh):
    in_specs = (
        P(("view", "point"), None, None, None),
        P(("view", "point"), None),
        P(("view", "point"), None, None),
        P(), P(), P(), P(),
    )
    out_specs = P(("view", "point"), None, None, None)
    body = functools.partial(shards, mesh.shape["view"], mesh.shape["point"])
    return jax.shard_map(body, mesh=mesh, in_specs=in_specs, out_specs=out_specs, check_vma=False)
```

```python
import functools

import jax
import jax.numpy as jnp
from jax import lax
from jax.experimental import pallas as pl
from jax.experimental.pallas import tpu as pltpu
from jax.sharding import PartitionSpec as P

VT_DEV = 4
PT_DEV = 4
MESH = pl.DeviceIdType.MESH
F32 = jnp.float32
BF16 = jnp.bfloat16


def wide(x, width):
    reps = width // x.shape[-1]
    return x if reps == 1 else jnp.concatenate([x] * reps, axis=-1)


def exchange_kernel(
    nv, np_, nk,
    tiles_ref, feat_ref, mask_ref, wself_ref, wcol_ref, wrow_ref, bias_ref,
    cur_out, colp_out, rowp_out,
    cur, pick, gather_mat, scatter_mat, col_send, rs_buf, f_send, f_buf, own_acc, b_send, b_buf, ag_send, ag_buf,
    row_acc, row_send, row_rs, row_ag_send, row_ag, row_p,
    ci_send, ci_buf, cf_send, cf_buf, ri_send, ri_buf, col_scale, row_scale, q_all,
    feat_sem, out_sem, rs_s, rs_r, f_s, f_r, b_s, b_r, ag_s, ag_r,
    rr_s, rr_r, ra_s, ra_r, ci_s, ci_r, cf_s, cf_r, ri_s, ri_r,
):
    a = lax.axis_index("view")
    b = lax.axis_index("point")
    slots, rows, cols, width = cur.shape
    layers = wself_ref.shape[0]
    chunk = cols // nk
    part = chunk // nv
    share = row_send.shape[1]
    nxt = lax.rem(b + 1, np_)
    prv = lax.rem(b + np_ - 1, np_)

    def remote(src, dst, ssem, rsem, va, pb):
        return pltpu.make_async_remote_copy(
            src_ref=src, dst_ref=dst, send_sem=ssem, recv_sem=rsem,
            device_id=(va, pb), device_id_type=MESH,
        )

    def view_at(o):
        return lax.rem(a + o, nv)

    def point_at(o):
        return lax.rem(b + o, np_)

    def rs_copy(k, o):
        return remote(col_send.at[k, view_at(o)], rs_buf.at[k, o - 1],
                      rs_s.at[k, o - 1], rs_r.at[k, o - 1], view_at(o), b)

    def ag_copy(k, o):
        return remote(ag_send.at[k, o - 1], ag_buf.at[k, o],
                      ag_s.at[k, o - 1], ag_r.at[k, o - 1], view_at(o), b)

    def f_copy(k):
        return remote(f_send.at[k], f_buf.at[k], f_s.at[k], f_r.at[k], a, nxt)

    def b_copy(k):
        return remote(b_send.at[k], b_buf.at[k], b_s.at[k], b_r.at[k], a, prv)

    def rr_copy(o):
        return remote(row_send.at[point_at(o)], row_rs.at[o - 1],
                      rr_s.at[o - 1], rr_r.at[o - 1], a, point_at(o))

    def ra_copy(o):
        return remote(row_ag_send, row_ag.at[o - 1], ra_s.at[o - 1], ra_r.at[o - 1], a, point_at(o))

    def ci_copy(o):
        return remote(ci_send.at[view_at(o)], ci_buf.at[o - 1],
                      ci_s.at[o - 1], ci_r.at[o - 1], view_at(o), b)

    def cf_copy():
        return remote(cf_send, cf_buf, cf_s.at[0], cf_r.at[0], a, nxt)

    def ri_copy(o):
        return remote(ri_send.at[point_at(o)], ri_buf.at[o - 1],
                      ri_s.at[o - 1], ri_r.at[o - 1], a, point_at(o))

    def feat_copy(k):
        span = pl.ds(k * chunk, chunk)
        return pltpu.make_async_copy(
            feat_ref.at[:, :, span, :], cur.at[:, :, span, :], feat_sem.at[k])

    for k in range(nk):
        feat_copy(k).start()

    barrier = pltpu.get_barrier_semaphore()
    for o in range(1, nv):
        pl.semaphore_signal(barrier, inc=1, device_id=(view_at(o), b), device_id_type=MESH)
    for o in range(1, np_):
        pl.semaphore_signal(barrier, inc=1, device_id=(a, point_at(o)), device_id_type=MESH)

    group = pick.shape[4] // chunk

    lanes = ci_send.shape[-1]
    per_part = nk * part
    for s in range(slots):
        m = mask_ref[s].astype(F32)
        ccount = jnp.broadcast_to(jnp.sum(m.T, axis=1, keepdims=True), (cols, lanes))
        q = jnp.full((8, lanes), tiles_ref[1, s], jnp.int32).astype(F32)
        for j in range(nv):
            for k in range(nk):
                at = k * chunk + j * part
                ci_send[j, s, k * part:(k + 1) * part, :] = ccount[at:at + part]
            ci_send[j, s, per_part:, :] = q
    for v in range(VT_DEV):
        total = jnp.zeros((rows, lanes), F32)
        for s in range(slots):
            rcount = jnp.broadcast_to(
                jnp.sum(mask_ref[s].astype(F32), axis=1, keepdims=True), (rows, lanes))
            hit = jnp.full((rows, lanes), tiles_ref[0, s], jnp.int32) == v
            total = total + jnp.where(hit, rcount, 0.0)
        for i in range(max(rows // share, 1)):
            at = v * rows + i * share
            ri_send[at // share] = total[i * share:(i + 1) * share]

    pl.semaphore_wait(barrier, nv - 1 + np_ - 1)
    for o in range(1, nv):
        ci_copy(o).start()
    for o in range(1, np_):
        ri_copy(o).start()

    def build_pick(s, carry):
        shape = (group, group * chunk)
        lane = lax.broadcasted_iota(jnp.int32, shape, 1)
        of_view = lane // chunk == lax.broadcasted_iota(jnp.int32, shape, 0)
        shape = (chunk, group * chunk)
        lane = lax.broadcasted_iota(jnp.int32, shape, 1)
        of_point = lane % chunk == lax.broadcasted_iota(jnp.int32, shape, 0)
        for g in range(rows // group):
            m = mask_ref[s, g * group:(g + 1) * group, :].astype(F32)
            for k in range(nk):
                tiled = jnp.concatenate([m[:, k * chunk:(k + 1) * chunk]] * group, axis=1)
                by_view = jnp.where(of_view, tiled, 0.0)
                flat = jnp.sum(by_view, axis=0, keepdims=True)
                by_point = jnp.where(of_point, jnp.broadcast_to(flat, shape), 0.0)
                both = jnp.concatenate([by_point, by_view, jnp.zeros_like(by_view)], axis=0)
                pick[s, k, g] = both.astype(BF16)
        return carry

    lax.fori_loop(0, slots, build_pick, 0)

    def sum_rows(k, s, value_of):
        col = jnp.zeros((chunk, width), F32)
        for g in range(rows // group):
            both = jnp.dot(pick[s, k, g], value_of(g), preferred_element_type=F32)
            col = col + both[:chunk]
            new = both[chunk:chunk + group]
            at = pl.ds(g * group, group)
            if k == 0:
                row_acc[s, at, :] = new
            else:
                row_acc[s, at, :] = row_acc[s, at, :] + new
        for j in range(nv):
            col_send[k, j, s] = col[j * part:(j + 1) * part]

    def entries(k, s, g):
        span = pl.ds(k * chunk, chunk)
        return cur[s, g * group:(g + 1) * group, span, :].reshape(group * chunk, width)

    def first_sums(k):
        def slot(s, carry):
            sum_rows(k, s, lambda g: entries(k, s, g))
            return carry
        lax.fori_loop(0, slots, slot, 0, unroll=4 if slots % 4 == 0 else 1)

    def layer_chunk(layer, k):
        span = pl.ds(k * chunk, chunk)

        def slot(s, carry):
            colp = jnp.concatenate(
                [ag_buf[k, lax.rem(a - j + nv, nv), s] for j in range(nv)], axis=0)
            v = tiles_ref[0, s]
            rowp = row_p[v]

            def value_of(g):
                z = jnp.dot(entries(k, s, g), wself_ref[layer], preferred_element_type=F32)
                z = z.reshape(group, chunk, width)
                y = z + colp[None] + rowp[g * group:(g + 1) * group][:, None, :]
                y = jnp.maximum(y, 0.0).astype(BF16)
                cur[s, g * group:(g + 1) * group, span, :] = y
                return y.reshape(group * chunk, width)
            sum_rows(k, s, value_of)
            return carry
        lax.fori_loop(0, slots, slot, 0, unroll=4 if slots % 4 == 0 else 1)

    def send_rows():
        for v in range(VT_DEV):
            total = jnp.zeros((rows, width), F32)
            for s in range(slots):
                hit = jnp.full((rows, width), tiles_ref[0, s], jnp.int32) == v
                total = total + jnp.where(hit, row_acc[s], 0.0)
            for i in range(max(rows // share, 1)):
                at = v * rows + i * share
                row_send[at // share] = total[i * share:(i + 1) * share]
        for o in range(1, np_):
            rr_copy(o).start()

    def send_cols(k):
        for o in range(1, nv):
            rs_copy(k, o).start()

    def halves(x):
        high = x.astype(BF16)
        return jnp.concatenate([high, (x - high.astype(F32)).astype(BF16)], axis=0)

    def picked(q, t, block):
        return jnp.where(q == float(t), block, 0.0)

    for k in range(nk):
        feat_copy(k).wait()
        first_sums(k)
        if k == nk - 1:
            send_rows()
        send_cols(k)

    for o in range(1, nv):
        ci_copy(o).wait()
    for s in range(slots):
        q_all[0, s] = wide(ci_send[a, s, per_part:, :], width)
        for o in range(1, nv):
            q_all[o, s] = wide(ci_buf[o - 1, s, per_part:, :], width)
    shape = scatter_mat.shape
    lane = lax.broadcasted_iota(jnp.int32, (8, shape[1]), 1) % (nv * slots * part)
    q_lane = jnp.zeros((8, shape[1]), F32)
    for o in range(nv):
        for s in range(slots):
            q = wide(ci_send[a, s, per_part:, :] if o == 0 else ci_buf[o - 1, s, per_part:, :],
                     shape[1])
            q_lane = jnp.where(lane // part == o * slots + s, q, q_lane)
    row = lax.broadcasted_iota(jnp.int32, shape, 0)
    lane = lax.broadcasted_iota(jnp.int32, shape, 1)
    q_lane = jnp.concatenate([q_lane] * (shape[0] // 8), axis=0)
    hit = (q_lane == (row // part).astype(F32)) & (row % part == lane % part)
    scatter_mat[...] = jnp.where(hit, 1.0, 0.0).astype(BF16)
    shape = (part, gather_mat.shape[1])
    lane = lax.broadcasted_iota(jnp.int32, shape, 1)
    same = lane % part == lax.broadcasted_iota(jnp.int32, shape, 0) % part
    tile = ((lane // part) % (2 * PT_DEV)).astype(F32)
    for o in range(nv):
        for s in range(slots):
            q = jnp.concatenate([q_all[(nv - o) % nv, s]] * (part // 8), axis=0)
            hit = (q[:, :shape[1]] == tile) & same
            at = (o * slots + s) * part
            gather_mat[at:at + part, :] = jnp.where(hit, 1.0, 0.0)
    for t in range(2 * PT_DEV):
        total = jnp.zeros((per_part, lanes), F32)
        for s in range(slots):
            for o in range(nv):
                block = ci_send.at[a] if o == 0 else ci_buf.at[o - 1]
                q = jnp.concatenate([block[s, per_part:, :]] * (per_part // 8), axis=0)
                total = total + picked(q, t, block[s, :per_part, :])
        if t < PT_DEV:
            col_scale[t] = total
        else:
            cf_send[t - PT_DEV] = total
    cf_copy().start()
    for o in range(1, np_):
        ri_copy(o).wait()
    total = ri_send[b]
    for o in range(1, np_):
        total = total + ri_buf[o - 1]
    row_scale[...] = wide(1.0 / jnp.sqrt(jnp.maximum(total, 1.0)), width)
    cf_copy().wait()
    for t in range(PT_DEV):
        total = col_scale[t] + cf_buf[t]
        col_scale[t] = 1.0 / jnp.sqrt(jnp.maximum(total, 1.0))

    def stage_sum(layer, k):
        for o in range(1, nv):
            rs_copy(k, o).wait()
        blocks = [col_send[k, a] if o == 0 else rs_buf[k, o - 1] for o in range(nv)]
        blocks = jnp.concatenate([x.reshape(slots * part, width) for x in blocks], axis=0)
        total = jnp.dot(scatter_mat[...], halves(blocks), preferred_element_type=F32)
        total = total.reshape(2 * PT_DEV, part, width)
        own_acc[k] = total[:PT_DEV]
        f_send[k] = total[PT_DEV:]
        f_copy(k).start()

    def stage_project(layer, k):
        f_copy(k).wait()
        scale = wide(col_scale[:, k * part:(k + 1) * part, :], width)
        term = ((own_acc[k] + f_buf[k]) * scale).reshape(PT_DEV * part, width).astype(BF16)
        out = jnp.dot(term, wcol_ref[layer], preferred_element_type=F32)
        b_send[k] = out.reshape(PT_DEV, part, width)
        b_copy(k).start()

    def stage_choose(layer, k):
        b_copy(k).wait()
        blocks = jnp.concatenate([b_send[k], b_buf[k]], axis=0)
        blocks = halves(blocks.reshape(2 * PT_DEV * part, width))
        chosen = jnp.dot(gather_mat[...].astype(BF16), blocks, preferred_element_type=F32)
        chosen = chosen.reshape(nv, slots, part, width)
        ag_buf[k, 0] = chosen[0]
        for o in range(1, nv):
            ag_send[k, o - 1] = chosen[o]
            ag_copy(k, o).start()

    def stage_row_project(layer):
        for o in range(1, np_):
            rr_copy(o).wait()
        total = row_send[b]
        for o in range(1, np_):
            total = total + row_rs[o - 1]
        term = (total * row_scale[...]).astype(BF16)
        row_ag_send[...] = (
            jnp.dot(term, wrow_ref[layer], preferred_element_type=F32)
            + bias_ref[pl.ds(layer, 1), :])
        for o in range(1, np_):
            ra_copy(o).start()

    def stage_row_collect(layer):
        for o in range(1, np_):
            ra_copy(o).wait()

        for j in range(np_):
            o = lax.rem(b - j + np_, np_)
            got = row_ag[jnp.maximum(o - 1, 0)]
            block = jnp.where(jnp.full(got.shape, o, jnp.int32) == 0, row_ag_send[...], got)
            at = j * share
            row_p[at // rows, at % rows:at % rows + share, :] = block

    def exchange(layer, carry):
        for wave in range(nk + 2):
            if wave < nk:
                stage_sum(layer, wave)
            if 0 <= wave - 1 < nk:
                stage_project(layer, wave - 1)
            if 0 <= wave - 2 < nk:
                stage_choose(layer, wave - 2)
            if wave == nk - 1:
                stage_row_project(layer)
        stage_row_collect(layer)
        for k in range(nk):
            for o in range(1, nv):
                ag_copy(k, o).wait()

            @pl.when(layer < layers - 1)
            def _():
                layer_chunk(layer, k)
                if k == nk - 1:
                    send_rows()
                send_cols(k)

        @pl.when(layer == layers - 2)
        def _():
            pltpu.make_async_copy(cur, cur_out, out_sem).start()
        return carry

    lax.fori_loop(0, layers, exchange, 0)
    for s in range(slots):
        rowp_out[s] = row_p[tiles_ref[0, s]]
        for k in range(nk):
            for j in range(nv):
                at = k * chunk + j * part
                colp_out[s, at:at + part, :] = ag_buf[k, lax.rem(a - j + nv, nv), s]
    pltpu.make_async_copy(cur, cur_out, out_sem).wait()


def last_layer_kernel(cur_ref, mask_ref, w_ref, colp_ref, rowp_ref, out_ref):
    _, group, cols, width = cur_ref.shape
    x = cur_ref[0].reshape(group * cols, width)
    mt = mask_ref[0].astype(F32).T
    for i in range(0, group, 2):
        z = jnp.dot(x[i * cols:(i + 2) * cols], w_ref[0], preferred_element_type=F32)
        for h in range(2):
            y = z[h * cols:(h + 1) * cols] + colp_ref[0] + rowp_ref[0, i + h:i + h + 1, :]
            m = jnp.broadcast_to(mt[:, i + h:i + h + 1], (cols, width))
            out_ref[0, i + h] = (jnp.maximum(y, 0.0) * m).astype(BF16)


def shards(nv, np_, features, tiles, masks, w_self, w_col, w_row, bias):
    slots, rows, cols, width = features.shape
    layers = w_self.shape[0]
    nk = max(cols // (8 * nv), 1)
    chunk = cols // nk
    part = chunk // nv
    share = VT_DEV * rows // np_
    lanes = 128
    group = 256 // chunk
    vmem = pltpu.VMEM
    dma = pltpu.SemaphoreType.DMA
    whole = pl.BlockSpec(memory_space=pltpu.VMEM)
    scratch = [
        vmem((slots, rows, cols, width), BF16),
        vmem((slots, nk, rows // group, chunk + 2 * group, group * chunk), BF16),
        vmem((nv * slots * part, 4 * PT_DEV * part), F32),
        vmem((2 * PT_DEV * part, 2 * nv * slots * part), BF16),
        vmem((nk, nv, slots, part, width), F32),
        vmem((nk, nv - 1, slots, part, width), F32),
        vmem((nk, PT_DEV, part, width), F32),
        vmem((nk, PT_DEV, part, width), F32),
        vmem((nk, PT_DEV, part, width), F32),
        vmem((nk, PT_DEV, part, width), F32),
        vmem((nk, PT_DEV, part, width), F32),
        vmem((nk, nv - 1, slots, part, width), F32),
        vmem((nk, nv, slots, part, width), F32),
        vmem((slots, rows, width), F32),
        vmem((np_, share, width), F32),
        vmem((np_ - 1, share, width), F32),
        vmem((share, width), F32),
        vmem((np_ - 1, share, width), F32),
        vmem((VT_DEV, rows, width), F32),
        vmem((nv, slots, nk * part + 8, lanes), F32),
        vmem((nv - 1, slots, nk * part + 8, lanes), F32),
        vmem((PT_DEV, nk * part, lanes), F32),
        vmem((PT_DEV, nk * part, lanes), F32),
        vmem((np_, share, lanes), F32),
        vmem((np_ - 1, share, lanes), F32),
        vmem((PT_DEV, nk * part, lanes), F32),
        vmem((share, width), F32),
        vmem((nv, slots, 8, width), F32),
        dma((nk,)),
        dma,
        dma((nk, nv - 1)), dma((nk, nv - 1)),
        dma((nk,)), dma((nk,)), dma((nk,)), dma((nk,)),
        dma((nk, nv - 1)), dma((nk, nv - 1)),
        dma((np_ - 1,)), dma((np_ - 1,)), dma((np_ - 1,)), dma((np_ - 1,)),
        dma((nv - 1,)), dma((nv - 1,)),
        dma((1,)), dma((1,)),
        dma((np_ - 1,)), dma((np_ - 1,)),
    ]
    current, colp, rowp = pl.pallas_call(
        functools.partial(exchange_kernel, nv, np_, nk),
        out_shape=(
            jax.ShapeDtypeStruct(features.shape, BF16),
            jax.ShapeDtypeStruct((slots, cols, width), F32),
            jax.ShapeDtypeStruct((slots, rows, width), F32),
        ),
        in_specs=[
            pl.BlockSpec(memory_space=pltpu.SMEM),
            pl.BlockSpec(memory_space=pl.ANY),
            whole, whole, whole, whole, whole,
        ],
        out_specs=(pl.BlockSpec(memory_space=pl.ANY), whole, whole),
        scratch_shapes=scratch,
        compiler_params=pltpu.CompilerParams(
            collective_id=0, has_side_effects=True, vmem_limit_bytes=60 * 1024 * 1024),
        name="exchange",
    )(tiles.T, features, masks, w_self, w_col, w_row, bias)
    group = rows
    return pl.pallas_call(
        last_layer_kernel,
        grid=(slots, rows // group),
        out_shape=jax.ShapeDtypeStruct(features.shape, BF16),
        in_specs=[
            pl.BlockSpec((1, group, cols, width), lambda s, g: (s, g, 0, 0)),
            pl.BlockSpec((1, group, cols), lambda s, g: (s, g, 0)),
            pl.BlockSpec((1, width, width), lambda s, g: (layers - 1, 0, 0)),
            pl.BlockSpec((1, cols, width), lambda s, g: (s, 0, 0)),
            pl.BlockSpec((1, group, width), lambda s, g: (s, g, 0)),
        ],
        out_specs=pl.BlockSpec((1, group, cols, width), lambda s, g: (s, g, 0, 0)),
        name="last_layer",
    )(current, masks, w_self, colp, rowp)


def solution(mesh):
    in_specs = (
        P(("view", "point"), None, None, None),
        P(("view", "point"), None),
        P(("view", "point"), None, None),
        P(), P(), P(), P(),
    )
    out_specs = P(("view", "point"), None, None, None)
    body = functools.partial(shards, mesh.shape["view"], mesh.shape["point"])
    return jax.shard_map(body, mesh=mesh, in_specs=in_specs, out_specs=out_specs, check_vma=False)
```
